32 devices in a mesh: rows: 16 (over z, y, x), rep: 2 (over core).
Axes of the slice: x: 2, y: 2, z: 4, core: 2. Of those that a mesh axis runs over, the one named last changes fastest.
Arguments:
- node_feats: bfloat16 [32768, 128], P('rows'), may hold values from -6 to 6
- w_in: bfloat16 [128, 256], replicated, may hold values from -0.5 to 0.5
- w_out: bfloat16 [256, 172], replicated
- labels: int32 [32768], P(('rows', 'rep')), may hold values from 0 to 171
- hub_rows: int32 [16, 2, 64], P('rows', 'rep'), may hold values from 0 to 2047, as said below
- send_rows: int32 [16, 2, 128], P('rows', 'rep'), may hold values from -1 to 2047, as said below
- adj_hub: bfloat16 [32768, 2, 1024], P('rows', 'rep'), may hold values from -0.125 to 0.125
- adj_sparse: bfloat16 [32768, 2, 128], P('rows', 'rep'), may hold values from -0.375 to 0.375
Outputs:
- logits: bfloat16 [32768, 172], P(('rows', 'rep'))
- grad_in: float32 [128, 256], replicated
- grad_out: float32 [256, 172], replicated
The draws below stay inside these ranges and needn't reach their ends.
Inputs may be any that keep to these rules, and one draw needn't show every extreme that they name: `hub_rows`: within each owner slab the 2 x 64 hub nodes are distinct. `send_rows`: for each source, half and destination the live slots (not -1) come first; their count is 1 to 8, and for every source and half some destination has all 8 slots live. A node may fill several slots.
All inputs are finite; a program needn't handle non-finite values.
Results may differ from the reference program's by a relative error of at most 0.0095.
The reference program's roundings to bfloat16 on the way (of `first`, `hidden` and `second`) count: a program that leaves them out, or rounds other values in their place, can miss the bound.
Values may be sent and summed in bfloat16 or wider, within the bound.
A program may use at most 128 MiB of HBM per device.

```python
import jax
import jax.numpy as jnp
from jax import lax

F = 128
HID = 256
C = 172
ROWS_DEV = 2048
HUBH = 64
CAPH = 8
NODES = 32768
HUB_ALL = 2048
SLOT_ALL = 256
N_ROWS = 16
N_REP = 2


def draw_w_out(key, part):
    base = jax.random.normal(key, (HID, C), jnp.float32) * HID ** (-0.5)
    return base.astype(jnp.bfloat16)


def draw_hub_rows(key, part):
    keys = jax.random.split(jax.random.fold_in(key, 21), N_ROWS)
    perms = jax.vmap(lambda single: jax.random.permutation(single, ROWS_DEV))(keys)
    return perms[:, :N_REP * HUBH].reshape(N_ROWS, N_REP, HUBH).astype(jnp.int32)


def draw_send_rows(key, part):
    key_count = jax.random.fold_in(key, 31)
    key_full = jax.random.fold_in(key, 32)
    key_rows = jax.random.fold_in(key, 33)
    counts = jax.random.randint(key_count, (N_ROWS, N_REP, N_ROWS), 1, CAPH + 1)
    full = jax.random.randint(key_full, (N_ROWS, N_REP, 1), 0, N_ROWS)
    counts = jnp.where(jnp.arange(N_ROWS)[None, None, :] == full, CAPH, counts)
    rows = jax.random.randint(key_rows, (N_ROWS, N_REP, N_ROWS, CAPH), 0, ROWS_DEV)
    live = jnp.arange(CAPH)[None, None, None, :] < counts[..., None]
    return jnp.where(live, rows, -1).reshape(N_ROWS, N_REP, N_ROWS * CAPH).astype(jnp.int32)


def touch_ends(drawn, stream_key, low, top_value):
    spot = [jax.random.randint(jax.random.fold_in(stream_key, axis), (), 0, length) for axis, length in enumerate(drawn.shape)]
    widest = drawn.shape.index(max(drawn.shape))
    beside = spot[:widest] + [(spot[widest] + 1) % drawn.shape[widest]] + spot[widest + 1:]
    return drawn.at[tuple(spot)].set(low).at[tuple(beside)].set(top_value)


def shard_levels(rng, shape, pieces, low, largest):
    loudness, own = 1.0, jax.random.fold_in(rng, 6)
    for dim, blocks in pieces:
        heights = jnp.exp(jax.random.uniform(jax.random.fold_in(own, dim), (blocks,), jnp.float32, low / len(pieces), largest / len(pieces)))
        loudness = loudness * jnp.repeat(heights, shape[dim] // blocks).reshape([-1 if axis == dim else 1 for axis in range(len(shape))])
    return loudness


def noise(stream_key, dims, scale, reach, shards=(), kind=jnp.bfloat16):
    drawn = jax.random.normal(stream_key, dims, jnp.float32) * scale
    if len(shards) > 0:
        drawn = shard_levels(stream_key, dims, shards, -0.22, 0.18) * drawn
    return jnp.clip(drawn, min=-reach, max=reach).astype(kind)


def setup_inputs(seed: int = 0) -> dict:
    arg_keys = jax.random.split(jax.random.key(seed), 9)
    return {
        "node_feats": noise(arg_keys[0], (NODES, F), 1.0, 6.0, ((0, 16),)),
        "w_in": noise(arg_keys[1], (F, HID), F ** -0.5, 0.5),
        "w_out": draw_w_out(jax.random.fold_in(arg_keys[8], 71), 0),
        "labels": touch_ends(jax.random.randint(arg_keys[3], (NODES,), 0, C), jax.random.fold_in(arg_keys[3], 1), 0, C - 1).astype(jnp.int32),
        "hub_rows": draw_hub_rows(jax.random.fold_in(arg_keys[8], 71), 0),
        "send_rows": draw_send_rows(jax.random.fold_in(arg_keys[8], 71), 0),
        "adj_hub": noise(arg_keys[6], (NODES, N_REP, N_ROWS * HUBH), HUB_ALL ** -0.5, 0.125, ((0, 16), (1, 2))),
        "adj_sparse": noise(arg_keys[7], (NODES, N_REP, N_ROWS * CAPH), SLOT_ALL ** -0.5, 0.375, ((0, 16), (1, 2))),
    }


def hub_node_ids(hub_rows):
    owners = jnp.arange(N_ROWS, dtype=jnp.int32)[:, None, None] * ROWS_DEV
    glob = owners + hub_rows
    return jnp.transpose(glob, (1, 0, 2)).reshape(N_REP, N_ROWS * HUBH)

def slot_node_ids(send_rows, slab):
    block = lax.dynamic_slice_in_dim(send_rows, (slab * CAPH).astype(jnp.int32), CAPH, 2)
    owners = jnp.arange(N_ROWS, dtype=jnp.int32)[:, None, None] * ROWS_DEV
    glob = jnp.transpose(owners + block, (1, 0, 2)).reshape(N_REP, N_ROWS * CAPH)
    live = jnp.transpose(block >= 0, (1, 0, 2)).reshape(N_REP, N_ROWS * CAPH)
    return (glob, live)

def aggregate(values, hub_rows, send_rows, adj_hub, adj_sparse):
    panel = values[hub_node_ids(hub_rows)]

    def one_slab(slab):
        start = (slab * ROWS_DEV).astype(jnp.int32)
        hub_block = lax.dynamic_slice_in_dim(adj_hub, start, ROWS_DEV, 0)
        sparse_block = lax.dynamic_slice_in_dim(adj_sparse, start, ROWS_DEV, 0)
        glob, live = slot_node_ids(send_rows, slab)
        rows = jnp.where(live[..., None], values[jnp.where(live, glob, 0)], jnp.zeros((), values.dtype))
        total = jnp.zeros((ROWS_DEV, values.shape[1]), jnp.float32)
        for member in range(N_REP):
            total = total + jnp.dot(hub_block[:, member, :], panel[member], preferred_element_type=jnp.float32)
            total = total + jnp.dot(sparse_block[:, member, :], rows[member], preferred_element_type=jnp.float32)
        return total
    out = lax.map(one_slab, jnp.arange(N_ROWS, dtype=jnp.int32))
    return out.reshape(NODES, values.shape[1])

def aggregate_t(grads, hub_rows, send_rows, adj_hub, adj_sparse):
    width = grads.shape[1]
    high = lax.Precision.HIGHEST

    def step(carry, slab):
        out, hub_grad = carry
        start = (slab * ROWS_DEV).astype(jnp.int32)
        hub_block = lax.dynamic_slice_in_dim(adj_hub, start, ROWS_DEV, 0).astype(jnp.float32)
        sparse_block = lax.dynamic_slice_in_dim(adj_sparse, start, ROWS_DEV, 0).astype(jnp.float32)
        local = lax.dynamic_slice_in_dim(grads, start, ROWS_DEV, 0)
        hub_terms = jnp.stack([jnp.dot(hub_block[:, member, :].T, local, precision=high) for member in range(N_REP)])
        slot_terms = jnp.stack([jnp.dot(sparse_block[:, member, :].T, local, precision=high) for member in range(N_REP)])
        glob, live = slot_node_ids(send_rows, slab)
        target = jnp.where(live, glob, NODES).reshape(-1)
        out = out.at[target].add(slot_terms.reshape(-1, width), mode='drop')
        return ((out, hub_grad + hub_terms), None)
    init = (jnp.zeros((NODES, width), jnp.float32), jnp.zeros((N_REP, N_ROWS * HUBH, width), jnp.float32))
    (out, hub_grad), _ = lax.scan(step, init, jnp.arange(N_ROWS, dtype=jnp.int32))
    out = out.at[hub_node_ids(hub_rows).reshape(-1)].add(hub_grad.reshape(-1, width))
    return out

def reference(node_feats, w_in, w_out, labels, hub_rows, send_rows, adj_hub, adj_sparse):
    high = lax.Precision.HIGHEST
    first = aggregate(node_feats, hub_rows, send_rows, adj_hub, adj_sparse).astype(jnp.bfloat16)
    pre = jnp.dot(first, w_in, preferred_element_type=jnp.float32)
    hidden = jnp.maximum(pre, 0.0).astype(jnp.bfloat16)
    second = aggregate(hidden, hub_rows, send_rows, adj_hub, adj_sparse).astype(jnp.bfloat16)
    scores = jnp.dot(second, w_out, preferred_element_type=jnp.float32)
    top = lax.optimization_barrier(jnp.max(scores, axis=1, keepdims=True))
    expo = jnp.exp(scores - top)
    probs = expo / lax.optimization_barrier(jnp.sum(expo, axis=1, keepdims=True))
    onehot = (labels[:, None] == jnp.arange(C, dtype=jnp.int32)[None, :]).astype(jnp.float32)
    dscore = (probs - onehot) * (1.0 / jnp.sqrt(jnp.float32(NODES)))
    grad_out = jnp.dot(second.astype(jnp.float32).T, dscore, precision=high)
    back = aggregate_t(dscore, hub_rows, send_rows, adj_hub, adj_sparse)
    dhidden = jnp.dot(back, w_out.astype(jnp.float32).T, precision=high)
    dpre = jnp.where(pre > 0, dhidden, jnp.zeros((), jnp.float32))
    grad_in = jnp.dot(first.astype(jnp.float32).T, dpre, precision=high)
    return (scores.astype(jnp.bfloat16), grad_in, grad_out)
```

```python
import jax
import jax.numpy as jnp
from jax import lax
from jax.sharding import PartitionSpec as P

F32 = jnp.float32
BF16 = jnp.bfloat16


def dot(a, b, dims=((1,), (0,))):
    return lax.dot_general(a, b, (dims, ((), ())), preferred_element_type=F32)


def split_dot(a, b, dims=((1,), (0,)), split=0):
    wide = (a, b)[split]
    high = wide.astype(BF16)
    low = (wide - high.astype(F32)).astype(BF16)
    if split == 0:
        return dot(high, b, dims) + dot(low, b, dims)
    return dot(a, high, dims) + dot(a, low, dims)


def on_device(node_feats, w_in, w_out, labels, hub_rows, send_rows, adj_hub, adj_sparse):
    nrows = lax.axis_size("rows")
    slab = node_feats.shape[0]
    total_nodes = slab * nrows
    hubs = hub_rows.shape[2]
    cap = send_rows.shape[2] // nrows
    hub_mat = adj_hub[:, 0, :]
    sparse_mat = adj_sparse[:, 0, :]
    iota = jnp.arange(slab, dtype=jnp.int32)
    mine = jnp.concatenate([hub_rows[0, 0], send_rows[0, 0]])
    both = lax.all_gather(mine, "rep", axis=0, tiled=True)
    pick = (both[:, None] == iota[None, :]).astype(BF16)
    pick_mine = (mine[:, None] == iota[None, :]).astype(BF16)
    hub_sel = dot(pick, hub_mat).astype(BF16)
    sparse_sel = dot(pick, sparse_mat).astype(BF16)

    def spread(rows):
        panel = lax.all_gather(rows[:hubs], "rows", axis=0, tiled=True)
        got = lax.all_to_all(
            rows[hubs:].reshape(nrows, cap, -1), "rows", split_axis=0, concat_axis=0, tiled=True
        )
        return panel, got.reshape(nrows * cap, -1)

    panel, got = spread(dot(pick_mine, node_feats).astype(BF16))
    part = dot(hub_sel, panel) + dot(sparse_sel, got)
    first = lax.psum_scatter(part, "rep", scatter_dimension=0, tiled=True).astype(BF16)
    pre = dot(first, w_in)
    hidden = jnp.maximum(pre, 0.0).astype(BF16)
    panel, got = spread(hidden)
    part = dot(hub_mat, panel) + dot(sparse_mat, got)
    second = lax.psum_scatter(part, "rep", scatter_dimension=0, tiled=True).astype(BF16)
    scores = dot(second, w_out)
    classes = scores.shape[1]
    top = jnp.max(scores, axis=1, keepdims=True)
    expo = jnp.exp(scores - top)
    probs = expo / jnp.sum(expo, axis=1, keepdims=True)
    onehot = (labels[:, None] == jnp.arange(classes, dtype=jnp.int32)[None, :]).astype(F32)
    dscore = (probs - onehot) * (1.0 / jnp.sqrt(F32(total_nodes)))
    grad_out = split_dot(second, dscore, ((0,), (0,)), 1)
    full = lax.all_gather(dscore.astype(BF16), "rep", axis=0, tiled=True)
    hub_terms = dot(hub_mat, full, ((0,), (0,)))
    slot_terms = dot(sparse_mat, full, ((0,), (0,))).astype(BF16).reshape(nrows, cap, classes)
    hub_grad = lax.psum_scatter(hub_terms, "rows", scatter_dimension=0, tiled=True)
    returned = lax.all_to_all(slot_terms, "rows", split_axis=0, concat_axis=0, tiled=True)
    back = jnp.concatenate([hub_grad, returned.reshape(nrows * cap, classes).astype(F32)])
    dhidden = split_dot(back, w_out, ((1,), (1,)))
    dpre = jnp.where(pre > 0, dhidden, 0.0)
    grad_in = split_dot(first, dpre, ((0,), (0,)), 1)
    grad_in, grad_out = lax.psum((grad_in, grad_out), ("rows", "rep"))
    return scores.astype(BF16), grad_in, grad_out


def solution(mesh):
    return jax.shard_map(
        on_device,
        mesh=mesh,
        in_specs=(
            P("rows", None),
            P(),
            P(),
            P(("rows", "rep")),
            P("rows", "rep", None),
            P("rows", "rep", None),
            P("rows", "rep", None),
            P("rows", "rep", None),
        ),
        out_specs=(P(("rows", "rep"), None), P(), P()),
        check_vma=False,
    )
```

```python
import functools
import math

import jax
import jax.numpy as jnp
from jax import lax
from jax.experimental import pallas as pl
from jax.experimental.pallas import tpu as pltpu
from jax.sharding import PartitionSpec as P

F32 = jnp.float32
BF16 = jnp.bfloat16
MESH = pl.DeviceIdType.MESH


def dot(a, b):
    return lax.dot_general(a, b, (((1,), (0,)), ((), ())), preferred_element_type=F32)


def parts(wide):
    high = wide.astype(BF16)
    return high, (wide - high.astype(F32)).astype(BF16)


def kernel(
    n, hubs, cap, classes, block,
    feats, w_in, w_out, labels, entries, hub_hbm, sparse_hbm,
    logits, grad_in, grad_out,
    hub, sparse, others, sel_hub, sel_sparse,
    hub_out_x, slot_out_x, panel_x, got_x,
    part_out, part_in,
    hub_out_h, slot_out_h, panel_h, got_h,
    half_out, half_in, second, secondT, w_pad, w_padT, lab,
    ds, dsT, terms, slot_terms, hub_back, slot_back,
    go_out, go_in, go_mid, go_mid_in, gi_out, gi_in, gi_mid, gi_mid_in,
    load_sem, rep_send, rep_recv, row_send, row_recv,
):
    me = lax.axis_index("rows")
    h = lax.axis_index("rep")
    partner = 1 - h
    slab, feat = feats.shape
    half = slab // 2
    nblk = half // block
    count = entries.shape[0]
    wide = w_pad.shape[1]

    loads = [
        pltpu.make_async_copy(hub_hbm, hub, load_sem.at[0]),
        pltpu.make_async_copy(sparse_hbm, sparse, load_sem.at[1]),
    ]
    for load in loads:
        load.start()

    barrier = pltpu.get_barrier_semaphore()

    def greet(k, _):
        pl.semaphore_signal(
            barrier, inc=1, device_id={"rows": lax.rem(me + k, n)}, device_id_type=MESH
        )
        return 0

    lax.fori_loop(1, n, greet, 0)
    pl.semaphore_signal(barrier, inc=1, device_id={"rep": partner}, device_id_type=MESH)

    def to_partner(src, dst, i):
        return pltpu.make_async_remote_copy(
            src_ref=src, dst_ref=dst, send_sem=rep_send.at[i], recv_sem=rep_recv.at[i],
            device_id={"rep": partner}, device_id_type=MESH,
        )

    def to_row(src, dst, kind, k, slot, peer):
        return pltpu.make_async_remote_copy(
            src_ref=src, dst_ref=dst, send_sem=row_send.at[kind, k],
            recv_sem=row_recv.at[kind, slot], device_id={"rows": peer}, device_id_type=MESH,
        )

    def exchange_start(flows):
        def body(k, _):
            peer = lax.rem(me + k, n)
            for kind, src, dst in flows:
                to_row(src(peer), dst(me), kind, k, me, peer).start()
            return 0

        lax.fori_loop(1, n, body, 0)

    def exchange_wait(flows):
        def body(k, _):
            peer = lax.rem(me + n - k, n)
            for kind, src, dst in flows:
                to_row(src(peer), dst(peer), kind, k, peer, peer).wait_recv()
            return 0

        def sent(k, _):
            peer = lax.rem(me + k, n)
            for kind, src, dst in flows:
                to_row(src(peer), dst(me), kind, k, me, peer).wait_send()
            return 0

        lax.fori_loop(1, n, body, 0)
        lax.fori_loop(1, n, sent, 0)

    def rows_at(ref, size):
        return lambda i: ref.at[pl.ds(pl.multiple_of(i * size, size), size)]

    def spread_flows(kind, hub_out, slot_out, panel, got):
        return [
            (kind, lambda i: hub_out, rows_at(panel, hubs)),
            (kind + 1, rows_at(slot_out, cap), rows_at(got, cap)),
        ]

    def keep_own(hub_out, slot_out, panel, got):
        panel[pl.ds(pl.multiple_of(me * hubs, hubs), hubs), :] = hub_out[...]
        at = pl.ds(pl.multiple_of(me * cap, cap), cap)
        got[at, :] = slot_out[at, :]

    iota = lax.broadcasted_iota(jnp.int32, (count, slab), 1)
    pick = jnp.where(entries[:, :1] == iota, 1.0, 0.0).astype(BF16)
    chosen = dot(pick, feats[...])
    hub_out_x[...] = chosen[:hubs].astype(BF16)
    slot_out_x[...] = chosen[hubs:]
    keep_own(hub_out_x, slot_out_x, panel_x, got_x)
    w_pad[...] = jnp.zeros_like(w_pad)
    w_pad[:, :classes] = w_out[...]

    pl.semaphore_wait(barrier, n)
    swap_list = to_partner(entries, others, 0)
    swap_list.start()
    flows_x = spread_flows(0, hub_out_x, slot_out_x, panel_x, got_x)
    exchange_start(flows_x)

    w_padT[...] = jnp.transpose(w_pad[...].astype(F32)).astype(BF16)
    lab[...] = jnp.transpose(jnp.broadcast_to(labels[...].astype(F32), (128, half)))
    for load in loads:
        load.wait()
    swap_list.wait()
    picks = jnp.concatenate(
        [pick, jnp.where(others[:, :1] == iota, 1.0, 0.0).astype(BF16)], axis=0
    )
    step = 256

    def select(j, _):
        at = pl.ds(pl.multiple_of(j * step, step), step)
        sel_hub[:, at] = dot(picks, hub[:, at]).astype(BF16)
        return 0

    lax.fori_loop(0, n * hubs // step, select, 0)
    sel_sparse[...] = dot(picks, sparse[...]).astype(BF16)

    exchange_wait(flows_x)
    got = got_x[...].astype(BF16)
    part_out[...] = dot(sel_hub[count:, :], panel_x[...]) + dot(sel_sparse[count:, :], got)
    swap_part = to_partner(part_out, part_in, 1)
    swap_part.start()
    part = dot(sel_hub[:count, :], panel_x[...]) + dot(sel_sparse[:count, :], got)
    swap_part.wait()
    first32 = (part + part_in[...]).astype(BF16).astype(F32)
    pre = dot(first32.astype(BF16), w_in[...])
    hidden = jnp.maximum(pre, 0.0).astype(BF16)
    hub_out_h[...] = hidden[:hubs]
    slot_out_h[...] = hidden[hubs:].astype(F32)
    flows_h = spread_flows(2, hub_out_h, slot_out_h, panel_h, got_h)
    exchange_start(flows_h)
    keep_own(hub_out_h, slot_out_h, panel_h, got_h)
    firstT = jnp.transpose(first32).astype(BF16)
    exchange_wait(flows_h)

    got2 = got_h[...].astype(BF16)

    def partial_at(row):
        at = pl.ds(pl.multiple_of(row, block), block)
        return dot(hub[at, :], panel_h[...]) + dot(sparse[at, :], got2)

    def swap_half(i):
        at = pl.ds(pl.multiple_of(i * block, block), block)
        return to_partner(half_out.at[at], half_in.at[at], 2 + i)

    def give(i, _):
        at = pl.ds(pl.multiple_of(i * block, block), block)
        half_out[at, :] = partial_at(partner * half + i * block)
        swap_half(i).start()
        return 0

    lax.fori_loop(0, nblk, give, 0)

    scale = 1.0 / math.sqrt(slab * n)
    column = lax.broadcasted_iota(jnp.int32, (block, wide), 1)

    column_wide = column.astype(F32)

    def swap_ds(i):
        return to_partner(dsT.at[h, i], dsT.at[h, i], 2 + nblk + i)

    def score(i, _):
        at = pl.ds(pl.multiple_of(i * block, block), block)
        mine = partial_at(h * half + i * block)
        swap_half(i).wait()
        sec = (mine + half_in[at, :]).astype(BF16)
        second[at, :] = sec
        scores = dot(sec, w_pad[...])
        logits[at, :] = scores[:, :classes].astype(BF16)
        inside = column < classes
        top = jnp.max(jnp.where(inside, scores, -jnp.inf), axis=1, keepdims=True)
        expo = jnp.where(inside, jnp.exp(jnp.where(inside, scores - top, 0.0)), 0.0)
        probs = expo / jnp.sum(expo, axis=1, keepdims=True)
        hot = jnp.where(lab[at, :1] == column_wide, 1.0, 0.0)
        dscore = (probs - hot) * scale
        dsT[h, i, :, :] = jnp.transpose(dscore).astype(BF16)
        swap_ds(i).start()
        ds[at, :] = dscore
        secondT[:, at] = jnp.transpose(sec.astype(F32)).astype(BF16)
        return 0

    lax.fori_loop(0, nblk, score, 0)

    ds_high, ds_low = parts(ds[...])
    grad_out_part = dot(secondT[...], ds_high) + dot(secondT[...], ds_low)

    def fill(out, value):
        size = out.shape[1]
        for i in range(n):
            out[i] = value[i * size : (i + 1) * size]

    def reduce_flow(kind, out, into):
        return [(kind, lambda i: out.at[i], lambda i: into.at[i])]

    fill(go_out, grad_out_part)
    go_flow = reduce_flow(6, go_out, go_in)
    exchange_start(go_flow)

    def swap_ds_wait(i, _):
        swap_ds(i).wait_send()
        pltpu.make_async_remote_copy(
            src_ref=dsT.at[partner, i], dst_ref=dsT.at[partner, i],
            send_sem=rep_send.at[2 + nblk + i], recv_sem=rep_recv.at[2 + nblk + i],
            device_id={"rep": partner}, device_id_type=MESH,
        ).wait_recv()
        return 0

    lax.fori_loop(0, nblk, swap_ds_wait, 0)

    def gather_dsT():
        return jnp.concatenate([dsT[j, i] for j in range(2) for i in range(nblk)], axis=1)

    full = gather_dsT()
    tcols = 256

    def term(j, _):
        at = pl.ds(pl.multiple_of(j * tcols, tcols), tcols)
        terms[at, :] = jnp.transpose(dot(full, hub[:, at])).astype(BF16)
        return 0

    lax.fori_loop(0, n * hubs // tcols, term, 0)
    slot_terms[...] = jnp.transpose(dot(full, sparse[...]))
    back_flows = [
        (4, rows_at(terms, hubs), lambda i: hub_back.at[i]),
        (5, rows_at(slot_terms, cap), rows_at(slot_back, cap)),
    ]
    exchange_start(back_flows)
    hub_back[me] = terms[pl.ds(pl.multiple_of(me * hubs, hubs), hubs), :]
    own_slots = pl.ds(pl.multiple_of(me * cap, cap), cap)
    slot_back[own_slots, :] = slot_terms[own_slots, :]

    def total_of(into, out, mid, mid_in, i):
        into[me] = out[me]
        mid[...] = jnp.sum(into[...], axis=0)
        swap = to_partner(mid, mid_in, i)
        swap.start()
        swap.wait()
        return mid[...] + mid_in[...]

    def share(kind, grad):
        return [(kind, lambda i: grad.at[me], lambda i: grad.at[i])]

    exchange_wait(go_flow)
    grad_out[me] = total_of(go_in, go_out, go_mid, go_mid_in, 2 + 2 * nblk)
    go_share = share(7, grad_out)
    exchange_start(go_share)

    exchange_wait(back_flows)
    back = jnp.concatenate(
        [jnp.sum(hub_back[...].astype(F32), axis=0), slot_back[...]], axis=0
    )
    back_high, back_low = parts(back)
    dhidden = dot(back_high, w_padT[...]) + dot(back_low, w_padT[...])
    dpre_high, dpre_low = parts(jnp.where(pre > 0, dhidden, 0.0))
    fill(gi_out, dot(firstT, dpre_high) + dot(firstT, dpre_low))
    gi_flow = reduce_flow(8, gi_out, gi_in)
    exchange_start(gi_flow)
    exchange_wait(go_share)
    exchange_wait(gi_flow)
    grad_in[me] = total_of(gi_in, gi_out, gi_mid, gi_mid_in, 3 + 2 * nblk)
    gi_share = share(9, grad_in)
    exchange_start(gi_share)
    exchange_wait(gi_share)


def on_device(node_feats, w_in, w_out, labels, hub_rows, send_rows, adj_hub, adj_sparse):
    n = lax.axis_size("rows")
    slab, feat = node_feats.shape
    half = slab // lax.axis_size("rep")
    hid, classes = w_out.shape
    wide = -(-classes // 128) * 128
    hubs, slots = hub_rows.shape[2], send_rows.shape[2]
    cap = slots // n
    count = hubs + slots
    panel = n * hubs
    block = min(256, half)
    nblk = half // block
    mine = jnp.concatenate([hub_rows[0, 0], send_rows[0, 0]])
    entries = jnp.broadcast_to(mine[:, None], (count, 128))
    vmem = pltpu.VMEM
    scratch = [
        vmem((slab, panel), BF16), vmem((slab, slots), BF16), vmem((count, 128), jnp.int32),
        vmem((2 * count, panel), BF16), vmem((2 * count, slots), BF16),
        vmem((hubs, feat), BF16), vmem((slots, feat), F32), vmem((panel, feat), BF16), vmem((slots, feat), F32),
        vmem((count, feat), F32), vmem((count, feat), F32),
        vmem((hubs, hid), BF16), vmem((slots, hid), F32), vmem((panel, hid), BF16), vmem((slots, hid), F32),
        vmem((half, hid), F32), vmem((half, hid), F32), vmem((half, hid), BF16), vmem((hid, half), BF16),
        vmem((hid, wide), BF16), vmem((wide, hid), BF16), vmem((half, 128), F32),
        vmem((half, wide), F32), vmem((2, nblk, wide, block), BF16),
        vmem((panel, wide), BF16), vmem((slots, wide), F32),
        vmem((n, hubs, wide), BF16), vmem((slots, wide), F32),
        vmem((n, hid // n, wide), F32), vmem((n, hid // n, wide), F32),
        vmem((hid // n, wide), F32), vmem((hid // n, wide), F32),
        vmem((n, feat // n, hid), F32), vmem((n, feat // n, hid), F32),
        vmem((feat // n, hid), F32), vmem((feat // n, hid), F32),
        pltpu.SemaphoreType.DMA((2,)),
        pltpu.SemaphoreType.DMA((4 + 2 * nblk,)), pltpu.SemaphoreType.DMA((4 + 2 * nblk,)),
        pltpu.SemaphoreType.DMA((10, n)), pltpu.SemaphoreType.DMA((10, n)),
    ]
    in_vmem = pl.BlockSpec(memory_space=vmem)
    anywhere = pl.BlockSpec(memory_space=pl.ANY)
    logits, grad_in, grad_out = pl.pallas_call(
        functools.partial(kernel, n, hubs, cap, classes, block),
        out_shape=(
            jax.ShapeDtypeStruct((half, classes), BF16),
            jax.ShapeDtypeStruct((n, feat // n, hid), F32),
            jax.ShapeDtypeStruct((n, hid // n, wide), F32),
        ),
        in_specs=[in_vmem] * 5 + [anywhere] * 2,
        out_specs=(in_vmem,) * 3,
        scratch_shapes=scratch,
        compiler_params=pltpu.CompilerParams(
            collective_id=0, has_side_effects=True, vmem_limit_bytes=64_000_000
        ),
        name="gcn",
    )(
        node_feats, w_in, w_out, labels.reshape(1, half), entries,
        adj_hub[:, 0, :], adj_sparse[:, 0, :],
    )
    return logits, grad_in.reshape(feat, hid), grad_out.reshape(hid, wide)[:, :classes]


def solution(mesh):
    return jax.shard_map(
        on_device,
        mesh=mesh,
        in_specs=(
            P("rows", None),
            P(),
            P(),
            P(("rows", "rep")),
            P("rows", "rep", None),
            P("rows", "rep", None),
            P("rows", "rep", None),
            P("rows", "rep", None),
        ),
        out_specs=(P(("rows", "rep"), None), P(), P()),
        check_vma=False,
    )
```

```python
import functools
import math

import jax
import jax.numpy as jnp
from jax import lax
from jax.experimental import pallas as pl
from jax.experimental.pallas import tpu as pltpu
from jax.sharding import PartitionSpec as P

F32 = jnp.float32
BF16 = jnp.bfloat16
MESH = pl.DeviceIdType.MESH


def dot(a, b):
    return lax.dot_general(a, b, (((1,), (0,)), ((), ())), preferred_element_type=F32)


def parts(wide):
    high = wide.astype(BF16)
    return high, (wide - high.astype(F32)).astype(BF16)


def kernel(
    n, hubs, cap, classes, block,
    feats, w_in, w_outT, labels, entries, hub_hbm, sparse_hbm,
    logits, grad_in, grad_out,
    hub, sparse, others, sel_hub, sel_sparse,
    hub_out_x, slot_out_x, panel_x, got_x,
    part_out, part_in,
    hub_out_h, slot_out_h, panel_h, got_h,
    half_out, half_in, second, ds_low, dsT, terms, slot_terms, hub_back, slot_back,
    go_out, go_in, go_mid, go_mid_in, go_all, gi_out, gi_in, gi_mid, gi_mid_in,
    load_sem, rep_send, rep_recv, row_send, row_recv, z_send, z_recv, p_send, p_recv,
):
    me = lax.axis_index("rows")
    h = lax.axis_index("rep")
    partner = 1 - h
    slab, feat = feats.shape
    half = slab // 2
    nblk = half // block
    count = entries.shape[0]
    deep = z_send.shape[1]
    plane = n // deep
    my_z, my_p = me // plane, lax.rem(me, plane)

    loads = [
        pltpu.make_async_copy(hub_hbm, hub, load_sem.at[0]),
        pltpu.make_async_copy(sparse_hbm, sparse, load_sem.at[1]),
    ]
    for load in loads:
        load.start()

    barrier = pltpu.get_barrier_semaphore()

    def greet(k, _):
        pl.semaphore_signal(
            barrier, inc=1, device_id={"rows": lax.rem(me + k, n)}, device_id_type=MESH
        )
        return 0

    lax.fori_loop(1, n, greet, 0)
    pl.semaphore_signal(barrier, inc=1, device_id={"rep": partner}, device_id_type=MESH)

    def to_partner(src, dst, i):
        return pltpu.make_async_remote_copy(
            src_ref=src, dst_ref=dst, send_sem=rep_send.at[i], recv_sem=rep_recv.at[i],
            device_id={"rep": partner}, device_id_type=MESH,
        )

    def to_row(src, dst, kind, k, slot, peer):
        return pltpu.make_async_remote_copy(
            src_ref=src, dst_ref=dst, send_sem=row_send.at[kind, k],
            recv_sem=row_recv.at[kind, slot], device_id={"rows": peer}, device_id_type=MESH,
        )

    def exchange_start(flows):
        def body(k, _):
            peer = lax.rem(me + k, n)
            for kind, src, dst in flows:
                to_row(src(peer), dst(me), kind, k, me, peer).start()
            return 0

        lax.fori_loop(1, n, body, 0)

    def exchange_wait(flows):
        def body(k, _):
            peer = lax.rem(me + n - k, n)
            for kind, src, dst in flows:
                to_row(src(peer), dst(peer), kind, k, peer, peer).wait_recv()
            return 0

        def sent(k, _):
            peer = lax.rem(me + k, n)
            for kind, src, dst in flows:
                to_row(src(peer), dst(me), kind, k, me, peer).wait_send()
            return 0

        lax.fori_loop(1, n, body, 0)
        lax.fori_loop(1, n, sent, 0)

    def rows_at(ref, size):
        return lambda i: ref.at[pl.ds(pl.multiple_of(i * size, size), size)]

    def z_copy(phase, src, panel, source, i, slot, peer):
        return pltpu.make_async_remote_copy(
            src_ref=src, dst_ref=rows_at(panel, hubs)(source), send_sem=z_send.at[phase, i],
            recv_sem=z_recv.at[phase, slot], device_id={"rows": peer}, device_id_type=MESH,
        )

    def p_copy(phase, src, panel, source, i, k, z, slot, peer):
        return pltpu.make_async_remote_copy(
            src_ref=src, dst_ref=rows_at(panel, hubs)(source), send_sem=p_send.at[phase, i, k],
            recv_sem=p_recv.at[phase, z, slot], device_id={"rows": peer}, device_id_type=MESH,
        )

    def pass_on(phase, src, panel, i, z, wait=False):
        def body(k, _):
            peer = my_z * plane + lax.rem(my_p + k, plane)
            copy = p_copy(phase, src, panel, z * plane + my_p, i, k, z, my_p, peer)
            copy.wait_send() if wait else copy.start()
            return 0

        lax.fori_loop(1, plane, body, 0)

    def gather_start(phase, hub_out, panel):
        def body(i, _):
            peer = lax.rem(my_z + i, deep) * plane + my_p
            z_copy(phase, hub_out, panel, me, i, my_z, peer).start()
            return 0

        lax.fori_loop(1, deep, body, 0)
        pass_on(phase, hub_out, panel, 0, my_z)

    def gather_wait(phase, hub_out, panel):
        def arrive(i, _):
            z = lax.rem(my_z + i, deep)
            source = z * plane + my_p
            z_copy(phase, hub_out, panel, source, i, z, source).wait_recv()
            pass_on(phase, rows_at(panel, hubs)(source), panel, i, z)
            return 0

        lax.fori_loop(1, deep, arrive, 0)

        def passed(i, _):
            z = lax.rem(my_z + i, deep)

            def body(k, _):
                slot = lax.rem(my_p + k, plane)
                p_copy(
                    phase, hub_out, panel, z * plane + slot, i, k, z, slot, my_z * plane + slot
                ).wait_recv()
                return 0

            lax.fori_loop(1, plane, body, 0)
            return 0

        lax.fori_loop(0, deep, passed, 0)

        def sent(i, _):
            peer = lax.rem(my_z + i, deep) * plane + my_p
            z_copy(phase, hub_out, panel, me, i, my_z, peer).wait_send()
            pass_on(phase, hub_out, panel, i, lax.rem(my_z + i, deep), True)
            return 0

        lax.fori_loop(1, deep, sent, 0)
        pass_on(phase, hub_out, panel, 0, my_z, True)

    def slot_flows(kind, slot_out, got):
        return [(kind, rows_at(slot_out, cap), rows_at(got, cap))]

    def keep_own(hub_out, slot_out, panel, got):
        panel[pl.ds(pl.multiple_of(me * hubs, hubs), hubs), :] = hub_out[...]
        at = pl.ds(pl.multiple_of(me * cap, cap), cap)
        got[at, :] = slot_out[at, :]

    iota = lax.broadcasted_iota(jnp.int32, (count, slab), 1)
    pick = jnp.where(entries[:, :1] == iota, 1.0, 0.0).astype(BF16)
    chosen = dot(pick, feats[...])
    hub_out_x[...] = chosen[:hubs].astype(BF16)
    slot_out_x[...] = chosen[hubs:]
    keep_own(hub_out_x, slot_out_x, panel_x, got_x)
    terms[...] = jnp.zeros_like(terms)
    slot_terms[...] = jnp.zeros_like(slot_terms)
    go_out[...] = jnp.zeros_like(go_out)

    pl.semaphore_wait(barrier, n)
    swap_list = to_partner(entries, others, 0)
    swap_list.start()
    flows_x = slot_flows(1, slot_out_x, got_x)
    gather_start(0, hub_out_x, panel_x)
    exchange_start(flows_x)

    for load in loads:
        load.wait()
    swap_list.wait()
    picks = jnp.concatenate(
        [pick, jnp.where(others[:, :1] == iota, 1.0, 0.0).astype(BF16)], axis=0
    )
    step = 256

    def select(j, _):
        at = pl.ds(pl.multiple_of(j * step, step), step)
        sel_hub[:, at] = dot(picks, hub[:, at]).astype(BF16)
        return 0

    lax.fori_loop(0, n * hubs // step, select, 0)
    sel_sparse[...] = dot(picks, sparse[...]).astype(BF16)

    gather_wait(0, hub_out_x, panel_x)
    exchange_wait(flows_x)
    got = got_x[...].astype(BF16)
    part_out[...] = dot(sel_hub[count:, :], panel_x[...]) + dot(sel_sparse[count:, :], got)
    swap_part = to_partner(part_out, part_in, 1)
    swap_part.start()
    part = dot(sel_hub[:count, :], panel_x[...]) + dot(sel_sparse[:count, :], got)
    swap_part.wait()
    first32 = (part + part_in[...]).astype(BF16).astype(F32)
    pre = dot(first32.astype(BF16), w_in[...])
    hidden = jnp.maximum(pre, 0.0).astype(BF16)
    hub_out_h[...] = hidden[:hubs]
    slot_out_h[...] = hidden[hubs:].astype(F32)
    flows_h = slot_flows(3, slot_out_h, got_h)
    gather_start(1, hub_out_h, panel_h)
    exchange_start(flows_h)
    keep_own(hub_out_h, slot_out_h, panel_h, got_h)
    firstT = jnp.transpose(first32).astype(BF16)
    gather_wait(1, hub_out_h, panel_h)
    exchange_wait(flows_h)

    got2 = got_h[...].astype(BF16)

    def partial_at(row):
        at = pl.ds(pl.multiple_of(row, block), block)
        return dot(hub[at, :], panel_h[...]) + dot(sparse[at, :], got2)

    def swap_half(i):
        at = pl.ds(pl.multiple_of(i * block, block), block)
        return to_partner(half_out.at[at], half_in.at[at], 2 + i)

    def give(i, _):
        at = pl.ds(pl.multiple_of(i * block, block), block)
        half_out[at, :] = partial_at(partner * half + i * block)
        swap_half(i).start()
        return 0

    lax.fori_loop(0, nblk, give, 0)

    scale = 1.0 / math.sqrt(slab * n)
    class_of = lax.broadcasted_iota(jnp.int32, (classes, block), 0)

    def swap_ds(i):
        return to_partner(dsT.at[h, i], dsT.at[h, i], 2 + nblk + i)

    def score(i, _):
        at = pl.ds(pl.multiple_of(i * block, block), block)
        mine = partial_at(h * half + i * block)
        swap_half(i).wait()
        sec = (mine + half_in[at, :]).astype(BF16)
        second[at, :] = sec
        scores = lax.dot_general(
            w_outT[...], sec, (((1,), (1,)), ((), ())), preferred_element_type=F32
        )
        logits[:, at] = scores.astype(BF16)
        expo = jnp.exp(scores - jnp.max(scores, axis=0, keepdims=True))
        probs = expo / jnp.sum(expo, axis=0, keepdims=True)
        hot = jnp.where(labels[:, at] == class_of, 1.0, 0.0)
        high, low = parts((probs - hot) * scale)
        dsT[h, i, :, :] = high
        swap_ds(i).start()
        ds_low[:, at] = low
        return 0

    lax.fori_loop(0, nblk, score, 0)

    ds_high = jnp.concatenate([dsT[h, i] for i in range(nblk)], axis=1)
    grad_out_part = dot(ds_high, second[...]) + dot(ds_low[...], second[...])

    def fill(out, value):
        size = out.shape[1]
        for i in range(n):
            piece = value[i * size : (i + 1) * size]
            if piece.shape[0]:
                out[i, : piece.shape[0], :] = piece

    def reduce_flow(kind, out, into):
        return [(kind, lambda i: out.at[i], lambda i: into.at[i])]

    fill(go_out, grad_out_part)
    go_flow = reduce_flow(6, go_out, go_in)
    exchange_start(go_flow)

    def swap_ds_wait(i, _):
        swap_ds(i).wait_send()
        pltpu.make_async_remote_copy(
            src_ref=dsT.at[partner, i], dst_ref=dsT.at[partner, i],
            send_sem=rep_send.at[2 + nblk + i], recv_sem=rep_recv.at[2 + nblk + i],
            device_id={"rep": partner}, device_id_type=MESH,
        ).wait_recv()
        return 0

    lax.fori_loop(0, nblk, swap_ds_wait, 0)

    def gather_dsT():
        return jnp.concatenate([dsT[j, i] for j in range(2) for i in range(nblk)], axis=1)

    full = gather_dsT()
    tcols = 256

    def term(j, _):
        at = pl.ds(pl.multiple_of(j * tcols, tcols), tcols)
        terms[at, :classes] = jnp.transpose(dot(full, hub[:, at])).astype(BF16)
        return 0

    lax.fori_loop(0, n * hubs // tcols, term, 0)
    slot_terms[:, :classes] = jnp.transpose(dot(full, sparse[...]))
    back_flows = [
        (4, rows_at(terms, hubs), lambda i: hub_back.at[i]),
        (5, rows_at(slot_terms, cap), rows_at(slot_back, cap)),
    ]
    exchange_start(back_flows)
    hub_back[me] = terms[pl.ds(pl.multiple_of(me * hubs, hubs), hubs), :]
    own_slots = pl.ds(pl.multiple_of(me * cap, cap), cap)
    slot_back[own_slots, :] = slot_terms[own_slots, :]

    def total_of(into, out, mid, mid_in, i):
        into[me] = out[me]
        mid[...] = jnp.sum(into[...], axis=0)
        swap = to_partner(mid, mid_in, i)
        swap.start()
        swap.wait()
        return mid[...] + mid_in[...]

    def share(kind, grad):
        return [(kind, lambda i: grad.at[me], lambda i: grad.at[i])]

    exchange_wait(go_flow)
    go_all[me] = total_of(go_in, go_out, go_mid, go_mid_in, 2 + 2 * nblk)
    go_share = share(7, go_all)
    exchange_start(go_share)

    exchange_wait(back_flows)
    back = jnp.concatenate(
        [jnp.sum(hub_back[...].astype(F32), axis=0), slot_back[...]], axis=0
    )
    back_high, back_low = parts(back[:, :classes])
    dhidden = dot(back_high, w_outT[...]) + dot(back_low, w_outT[...])
    dpre_high, dpre_low = parts(jnp.where(pre > 0, dhidden, 0.0))
    fill(gi_out, dot(firstT, dpre_high) + dot(firstT, dpre_low))
    gi_flow = reduce_flow(8, gi_out, gi_in)
    exchange_start(gi_flow)
    exchange_wait(go_share)
    exchange_wait(gi_flow)
    grad_in[me] = total_of(gi_in, gi_out, gi_mid, gi_mid_in, 3 + 2 * nblk)
    gi_share = share(9, grad_in)
    exchange_start(gi_share)
    go_rows = go_all.shape[1]
    for i in range(n):
        size = min(go_rows, classes - i * go_rows)
        if size > 0:
            grad_out[pl.ds(i * go_rows, size), :] = go_all[i, :size, :]
    exchange_wait(gi_share)


def on_device(node_feats, w_in, w_out, labels, hub_rows, send_rows, adj_hub, adj_sparse):
    n = lax.axis_size("rows")
    slab, feat = node_feats.shape
    half = slab // lax.axis_size("rep")
    hid, classes = w_out.shape
    wide = -(-classes // 128) * 128
    hubs, slots = hub_rows.shape[2], send_rows.shape[2]
    cap = slots // n
    count = hubs + slots
    panel = n * hubs
    block = min(256, half)
    piece = -(-classes // (8 * n)) * 8
    deep = 4 if n % 4 == 0 else 1
    nblk = half // block
    mine = jnp.concatenate([hub_rows[0, 0], send_rows[0, 0]])
    entries = jnp.broadcast_to(mine[:, None], (count, 128))
    vmem = pltpu.VMEM
    scratch = [
        vmem((slab, panel), BF16), vmem((slab, slots), BF16), vmem((count, 128), jnp.int32),
        vmem((2 * count, panel), BF16), vmem((2 * count, slots), BF16),
        vmem((hubs, feat), BF16), vmem((slots, feat), F32), vmem((panel, feat), BF16), vmem((slots, feat), F32),
        vmem((count, feat), F32), vmem((count, feat), F32),
        vmem((hubs, hid), BF16), vmem((slots, hid), F32), vmem((panel, hid), BF16), vmem((slots, hid), F32),
        vmem((half, hid), F32), vmem((half, hid), F32), vmem((half, hid), BF16),
        vmem((classes, half), BF16), vmem((2, nblk, classes, block), BF16),
        vmem((panel, wide), BF16), vmem((slots, wide), F32),
        vmem((n, hubs, wide), BF16), vmem((slots, wide), F32),
        vmem((n, piece, hid), F32), vmem((n, piece, hid), F32),
        vmem((piece, hid), F32), vmem((piece, hid), F32), vmem((n, piece, hid), F32),
        vmem((n, feat // n, hid), F32), vmem((n, feat // n, hid), F32),
        vmem((feat // n, hid), F32), vmem((feat // n, hid), F32),
        pltpu.SemaphoreType.DMA((2,)),
        pltpu.SemaphoreType.DMA((4 + 2 * nblk,)), pltpu.SemaphoreType.DMA((4 + 2 * nblk,)),
        pltpu.SemaphoreType.DMA((10, n)), pltpu.SemaphoreType.DMA((10, n)),
        pltpu.SemaphoreType.DMA((2, deep)), pltpu.SemaphoreType.DMA((2, deep)),
        pltpu.SemaphoreType.DMA((2, deep, n // deep)), pltpu.SemaphoreType.DMA((2, deep, n // deep)),
    ]
    in_vmem = pl.BlockSpec(memory_space=vmem)
    anywhere = pl.BlockSpec(memory_space=pl.ANY)
    logits, grad_in, grad_out = pl.pallas_call(
        functools.partial(kernel, n, hubs, cap, classes, block),
        out_shape=(
            jax.ShapeDtypeStruct((classes, half), BF16),
            jax.ShapeDtypeStruct((n, feat // n, hid), F32),
            jax.ShapeDtypeStruct((classes, hid), F32),
        ),
        in_specs=[in_vmem] * 5 + [anywhere] * 2,
        out_specs=(in_vmem,) * 3,
        scratch_shapes=scratch,
        compiler_params=pltpu.CompilerParams(
            collective_id=0, has_side_effects=True, vmem_limit_bytes=64_000_000
        ),
        name="gcn",
    )(
        node_feats, w_in, w_out.T, labels.reshape(1, half), entries,
        adj_hub[:, 0, :], adj_sparse[:, 0, :],
    )
    return logits.T, grad_in.reshape(feat, hid), grad_out.T


def solution(mesh):
    return jax.shard_map(
        on_device,
        mesh=mesh,
        in_specs=(
            P("rows", None),
            P(),
            P(),
            P(("rows", "rep")),
            P("rows", "rep", None),
            P("rows", "rep", None),
            P("rows", "rep", None),
            P("rows", "rep", None),
        ),
        out_specs=(P(("rows", "rep"), None), P(), P()),
        check_vma=False,
    )
```
